32 devices in a mesh: blk: 4 (over y, core), grp: 8 (over z, x).
Axes of the slice: x: 2, y: 2, z: 4, core: 2. Of those that a mesh axis runs over, the one named last changes fastest.
Arguments:
- a_blocks: bfloat16 [64, 27, 64, 64], P(('blk', 'grp')), may hold values from -0.75 to 0.75
- a_slot: int32 [64, 27], P(('blk', 'grp')), may hold values from 0 to 13
- import_rows: int32 [32, 7, 2], P(('blk', 'grp')), may hold values from 0 to 1
- p_blocks: bfloat16 [64, 2, 64, 64], P(('blk', 'grp')), may hold values from -0.75 to 0.75
- next_mask: int32 [64], P(('blk', 'grp')), may hold values 0 or 1
Outputs:
- coarse: bfloat16 [2048, 1344], P(('blk', 'grp'))
The draws below stay inside these ranges and needn't reach their ends.
All inputs are finite; a program needn't handle non-finite values. No bound on the sum of `next_mask` on one device may be relied on, other than what follows from the above.
Results may differ from the reference program's by a relative error of at most 0.006.
Values may be sent and summed in bfloat16 or wider, within the bound.
No kernel may reach another device: no remote copies, remote signals or barrier semaphores. Data moves between devices by JAX's collectives and lax.ppermute only.
A program may use at most 64 MiB of HBM per device.

```python
import jax
import jax.numpy as jnp
from jax import lax

BS = 64
KA = 27
CAP = 2
ROWS_DEV = 2
NB = 7
FINE_ROWS = 64
N_BLK = 4
N_GRP = 8
DEVICES = 32


def place_ends(values, own_key, low, high):
    shape = values.shape
    spot = [jax.random.randint(jax.random.fold_in(own_key, axis), (), 0, shape[axis]) for axis in range(len(shape))]
    values = values.at[tuple(spot)].set(low)
    longest = shape.index(max(shape))
    spot[longest] = (spot[longest] + 1) % shape[longest]
    return values.at[tuple(spot)].set(high)


def levels(own_key, shape, pieces, least, top_value):
    def one(position, shards_of):
        draws = jax.random.uniform(jax.random.fold_in(jax.random.fold_in(own_key, 6), position), (shards_of,), jnp.float32, least / len(pieces), top_value / len(pieces))
        return jnp.repeat(jnp.exp(draws), shape[position] // shards_of).reshape((-1,) + (1,) * (len(shape) - position - 1))

    level = one(*pieces[0])
    for cut in pieces[1:]:
        level = level * one(*cut)
    return level


def scatter_about(key, shape, scale, most, cuts=(), kind=jnp.bfloat16):
    entries = scale * jax.random.normal(key, shape, jnp.float32)
    if cuts:
        entries = entries * levels(key, shape, cuts, -0.22, 0.18)
    return jnp.clip(entries, -most, most).astype(kind)


def setup_inputs(seed: int = 0) -> dict:
    seeds = jax.random.split(jax.random.key(seed), 6)
    a_blocks = scatter_about(seeds[0], (FINE_ROWS, KA, BS, BS), BS ** -0.5, 0.75, ((0, 32),))
    a_slot = place_ends(jax.random.randint(seeds[1], (FINE_ROWS, KA), 0, NB * CAP), jax.random.fold_in(seeds[1], 1), 0, (NB * CAP) - 1).astype(jnp.int32)
    import_rows = place_ends(jax.random.randint(seeds[2], (DEVICES, NB, CAP), 0, ROWS_DEV), jax.random.fold_in(seeds[2], 1), 0, ROWS_DEV - 1).astype(jnp.int32)
    p_blocks = scatter_about(seeds[3], (FINE_ROWS, 2, BS, BS), BS ** -0.5, 0.75, ((0, 32),))
    next_mask = place_ends((jax.random.randint(seeds[4], (FINE_ROWS,), 0, 2) < 1).astype(jnp.int32), jax.random.fold_in(seeds[4], 1), 0, 1)
    return {"a_blocks": a_blocks, "a_slot": a_slot, "import_rows": import_rows, "p_blocks": p_blocks, "next_mask": next_mask}


def group_terms(blocks, slot_ids, imports, pm_group):
    products = jnp.einsum('groim,grkij->grkomj', pm_group.astype(jnp.float32), blocks.astype(jnp.float32))
    segment_ids = (jnp.arange(N_GRP, dtype=jnp.int32)[:, None, None] * (NB * CAP) + slot_ids).reshape(-1)
    left_factor = jax.ops.segment_sum(products.reshape(-1, 2, BS, BS), segment_ids, num_segments=N_GRP * NB * CAP)
    left_factor = left_factor.astype(jnp.bfloat16).reshape(N_GRP, NB, CAP, 2 * BS, BS)
    owner_index = (jnp.arange(N_GRP, dtype=jnp.int32)[:, None] + jnp.arange(NB, dtype=jnp.int32)[None, :] - NB // 2) % N_GRP
    imported = pm_group[owner_index[:, :, None], imports]
    return jnp.einsum('gdcxj,gdcojn->gxdon', left_factor.astype(jnp.float32), imported.astype(jnp.float32))


def reference(a_blocks, a_slot, import_rows, p_blocks, next_mask):
    row_scale = jnp.stack([jnp.ones_like(next_mask), next_mask], axis=1).astype(jnp.bfloat16)
    masked = p_blocks * row_scale[:, :, None, None]
    blocks_all = a_blocks.reshape(N_BLK, N_GRP, ROWS_DEV, KA, BS, BS)
    slots_all = a_slot.reshape(N_BLK, N_GRP, ROWS_DEV, KA)
    imports_all = import_rows.reshape(N_BLK, N_GRP, NB, CAP)
    masked_all = masked.reshape(N_BLK, N_GRP, ROWS_DEV, 2, BS, BS)

    def terms_of(group_index):
        return group_terms(blocks_all[group_index], slots_all[group_index], imports_all[group_index], masked_all[group_index])

    wrapped = terms_of(N_BLK - 1)[:, BS:]

    def advance(prior_next, group_index):
        partial_value = terms_of(group_index)
        own_part = partial_value[:, :BS]
        assembled = jnp.stack([prior_next[:, :, :, 0], prior_next[:, :, :, 1] + own_part[:, :, :, 0], own_part[:, :, :, 1]], axis=3)
        return partial_value[:, BS:], assembled.astype(jnp.bfloat16).reshape(N_GRP * BS, NB * 3 * BS)

    _, stacked = lax.scan(advance, wrapped, jnp.arange(N_BLK, dtype=jnp.int32))
    return stacked.reshape(N_BLK * N_GRP * BS, NB * 3 * BS)
```

```python
import functools

import jax
import jax.numpy as jnp
from jax import lax
from jax.experimental import pallas as pl
from jax.experimental.pallas import tpu as pltpu
from jax.sharding import PartitionSpec as P

VMEM = pl.BlockSpec(memory_space=pltpu.VMEM)
SMEM = pl.BlockSpec(memory_space=pltpu.SMEM)


def near(value):
    return pltpu.with_memory_space_constraint(value, pltpu.VMEM)


def pack_kernel(mask_ref, p_ref, out_ref):
    rows, _, size, _ = p_ref.shape
    for r in range(rows):
        second = p_ref[r, 1].astype(jnp.float32) * mask_ref[r].astype(jnp.float32)
        out_ref[r * size : (r + 1) * size, :] = jnp.concatenate(
            [p_ref[r, 0], second.astype(jnp.bfloat16)], axis=1
        )


def left_kernel(slot_ref, wanted_ref, packed_ref, a_ref, out_ref, *sums):
    rows, stencil, size, _ = a_ref.shape
    caps = wanted_ref.shape[2]
    for r in range(rows):
        sums[r][...] = jnp.zeros_like(sums[r])
    for k in range(stencil):
        for r in range(rows):
            slot = slot_ref[r, k]
            place, c = slot // caps, slot % caps
            t = place * rows + wanted_ref[0, place, c]
            sums[r][t] += a_ref[r, k].astype(jnp.float32)
    turned = packed_ref[...].T
    for d in range(out_ref.shape[0]):
        x = jnp.concatenate(
            [
                jnp.concatenate([sums[r][d * rows + q] for r in range(rows)], axis=0)
                for q in range(rows)
            ],
            axis=1,
        )
        high = x.astype(jnp.bfloat16)
        low = (x - high.astype(jnp.float32)).astype(jnp.bfloat16)
        value = jnp.dot(turned, high, preferred_element_type=jnp.float32)
        value += jnp.dot(turned, low, preferred_element_type=jnp.float32)
        out_ref[d] = value.astype(jnp.bfloat16)


def product_kernel(sources, group, left_ref, *refs):
    own_ref, next_ref = refs[-2:]
    neighbours, size, _ = own_ref.shape
    g = lax.axis_index("grp")
    for held, ref in zip(sources, refs[:-2]):
        for i, source in held:
            d = lax.rem(source(g) - g + neighbours // 2 + group, group)
            factor = ref[...] if i is None else ref[i]
            value = jnp.dot(left_ref[d], factor, preferred_element_type=jnp.float32)
            own_ref[d] = value[:size]
            next_ref[d] = value[size:].astype(jnp.bfloat16)


def output_kernel(x_ref, o_ref, out_ref):
    neighbours, size, width = x_ref.shape
    half = width // 2
    lower = lax.broadcasted_iota(jnp.int32, (size, width), 1) < half
    for d in range(0, neighbours, 2):
        at = d * 3 * half
        x, o = x_ref[d].astype(jnp.float32), o_ref[d]
        turned = pltpu.roll(o, half, 1)
        first = jnp.where(lower, x, x + turned)
        out_ref[:, at : at + width] = first.astype(jnp.bfloat16)
        if d + 1 < neighbours:
            y, q = x_ref[d + 1].astype(jnp.float32), o_ref[d + 1]
            moved = pltpu.roll(y, half, 1)
            second = jnp.where(lower, turned, moved)
            third = jnp.where(lower, q + moved, q)
            out_ref[:, at + width : at + 2 * width] = second.astype(jnp.bfloat16)
            out_ref[:, at + 2 * width : at + 3 * width] = third.astype(jnp.bfloat16)
        else:
            out_ref[:, at + width : at + 3 * half] = turned[:, :half].astype(jnp.bfloat16)


def shards(a_blocks, a_slot, import_rows, p_blocks, next_mask):
    rows, stencil, size, _ = a_blocks.shape
    neighbours = import_rows.shape[1]
    group = lax.axis_size("grp")

    def move(value, axis, place):
        route = [(i, place(i)) for i in range(lax.axis_size(axis))]
        return lax.ppermute(value, axis, route)

    packed = pl.pallas_call(
        pack_kernel,
        out_shape=pltpu.VMEM((rows * size, 2 * size), jnp.bfloat16),
        in_specs=[SMEM, VMEM],
        out_specs=VMEM,
    )(next_mask, p_blocks)
    left = pl.pallas_call(
        left_kernel,
        out_shape=pltpu.VMEM((neighbours, 2 * size, rows * size), jnp.bfloat16),
        in_specs=[SMEM, SMEM, VMEM, VMEM],
        out_specs=VMEM,
        scratch_shapes=[pltpu.VMEM((neighbours * rows, size, size), jnp.float32)] * rows,
    )(a_slot, import_rows, near(packed), near(a_blocks))

    came, sources = [packed], [[(None, lambda g: g)]]
    if neighbours == group - 1 and group & (group - 1) == 0:
        half = group // 2
        across = move(packed, "grp", lambda g: g ^ half)
        pair = jnp.stack([packed, across])
        for m in range(1, half):
            came.append(move(pair, "grp", lambda g, m=m: g ^ m))
            sources.append([(0, lambda g, m=m: g ^ m), (1, lambda g, m=m: g ^ m ^ half)])
    else:
        for k in range(1, neighbours // 2 + 1):
            for s in (k, -k):
                came.append(move(packed, "grp", lambda g, s=s: (g - s) % group))
                sources.append([(None, lambda g, s=s: g + s)])

    own, onward = pl.pallas_call(
        functools.partial(product_kernel, sources, group),
        out_shape=[
            pltpu.VMEM((neighbours, size, 2 * size), jnp.float32),
            pltpu.VMEM((neighbours, size, 2 * size), jnp.bfloat16),
        ],
        in_specs=[VMEM] * (len(came) + 1),
        out_specs=[VMEM] * 2,
    )(near(left), *[near(c) for c in came])
    parts = lax.axis_size("blk")
    prior = move(onward, "blk", lambda b: (b + 1) % parts)
    return pl.pallas_call(
        output_kernel,
        out_shape=jax.ShapeDtypeStruct((size, neighbours * 3 * size), jnp.bfloat16),
        in_specs=[VMEM] * 2,
        out_specs=VMEM,
    )(near(prior), near(own))


def solution(mesh):
    in_specs = (
        P(("blk", "grp"), None, None, None),
        P(("blk", "grp"), None),
        P(("blk", "grp"), None, None),
        P(("blk", "grp"), None, None, None),
        P(("blk", "grp")),
    )
    out_specs = P(("blk", "grp"), None)
    return jax.shard_map(shards, mesh=mesh, in_specs=in_specs, out_specs=out_specs, check_vma=False)
```

```python
import functools

import jax
import jax.numpy as jnp
from jax import lax
from jax.experimental import pallas as pl
from jax.experimental.pallas import tpu as pltpu
from jax.sharding import PartitionSpec as P

VMEM = pl.BlockSpec(memory_space=pltpu.VMEM)
SMEM = pl.BlockSpec(memory_space=pltpu.SMEM)


def near(value):
    return pltpu.with_memory_space_constraint(value, pltpu.VMEM)


def pack_kernel(mask_ref, p_ref, out_ref):
    rows, _, size, _ = p_ref.shape
    for r in range(rows):
        second = p_ref[r, 1].astype(jnp.float32) * mask_ref[r].astype(jnp.float32)
        out_ref[r * size : (r + 1) * size, :] = jnp.concatenate(
            [p_ref[r, 0], second.astype(jnp.bfloat16)], axis=1
        )


def left_kernel(slot_ref, wanted_ref, packed_ref, a_ref, out_ref, *sums):
    rows, stencil, size, _ = a_ref.shape
    caps = wanted_ref.shape[0]
    for r in range(rows):
        sums[r][...] = jnp.zeros_like(sums[r])
    for k in range(stencil):
        for r in range(rows):
            slot = slot_ref[r, k]
            place, c = slot // caps, slot % caps
            t = place * rows + wanted_ref[c, place]
            sums[r][t] += a_ref[r, k].astype(jnp.float32)
    turned = packed_ref[...].T
    for d in range(out_ref.shape[0]):
        x = jnp.concatenate(
            [
                jnp.concatenate([sums[r][d * rows + q] for r in range(rows)], axis=0)
                for q in range(rows)
            ],
            axis=1,
        )
        high = x.astype(jnp.bfloat16)
        low = (x - high.astype(jnp.float32)).astype(jnp.bfloat16)
        value = jnp.dot(turned, high, preferred_element_type=jnp.float32)
        value += jnp.dot(turned, low, preferred_element_type=jnp.float32)
        out_ref[d] = value.astype(jnp.bfloat16)


def product_kernel(plan, left_ref, *refs):
    own_ref, next_ref = refs[-2:]
    size = own_ref.shape[1]
    g = lax.axis_index("grp")
    at = 0
    for places, ref in zip(plan, refs[:-2]):
        for i, place in enumerate(places):
            factor = ref[...] if len(ref.shape) == 2 else ref[i]
            if place is None:
                continue
            value = jnp.dot(left_ref[place(g)], factor, preferred_element_type=jnp.float32)
            own_ref[at] = value[:size]
            next_ref[at] = value[size:].astype(jnp.bfloat16)
            at += 1


def output_kernel(entry_of, neighbours, counts, *refs):
    pieces, owns = refs[: len(counts)], refs[len(counts) : 2 * len(counts)]
    out_ref, prior, own = refs[2 * len(counts) :]
    size, width = own.shape[1:]
    half = width // 2
    lower = lax.broadcasted_iota(jnp.int32, (size, width), 1) < half
    g = lax.axis_index("grp")
    for piece, mine, entries in zip(pieces, owns, counts):
        for i, e in enumerate(entries):
            prior[e] = piece[i].astype(jnp.float32)
            own[e] = mine[i]
    for d in range(0, neighbours, 2):
        at = d * 3 * half
        e = entry_of(d, g)
        x, o = prior[e], own[e]
        turned = pltpu.roll(o, half, 1)
        first = jnp.where(lower, x, x + turned)
        out_ref[:, at : at + width] = first.astype(jnp.bfloat16)
        if d + 1 < neighbours:
            e = entry_of(d + 1, g)
            y, q = prior[e], own[e]
            moved = pltpu.roll(y, half, 1)
            second = jnp.where(lower, turned, moved)
            third = jnp.where(lower, q + moved, q)
            out_ref[:, at + width : at + 2 * width] = second.astype(jnp.bfloat16)
            out_ref[:, at + 2 * width : at + 3 * width] = third.astype(jnp.bfloat16)
        else:
            out_ref[:, at + width : at + 3 * half] = turned[:, :half].astype(jnp.bfloat16)


def shards(a_blocks, a_slot, import_rows, p_blocks, next_mask):
    rows, stencil, size, _ = a_blocks.shape
    neighbours = import_rows.shape[1]
    middle = neighbours // 2
    group, parts = lax.axis_size("grp"), lax.axis_size("blk")

    def move(value, axis, place):
        route = [(i, place(i)) for i in range(lax.axis_size(axis))]
        return lax.ppermute(value, axis, route)

    packed = pl.pallas_call(
        pack_kernel,
        out_shape=pltpu.VMEM((rows * size, 2 * size), jnp.bfloat16),
        in_specs=[SMEM, VMEM],
        out_specs=VMEM,
    )(next_mask, p_blocks)
    left = pl.pallas_call(
        left_kernel,
        out_shape=pltpu.VMEM((neighbours, 2 * size, rows * size), jnp.bfloat16),
        in_specs=[SMEM, SMEM, VMEM, VMEM],
        out_specs=VMEM,
        scratch_shapes=[pltpu.VMEM((neighbours * rows, size, size), jnp.float32)] * rows,
    )(a_slot, import_rows[0].T, near(packed), a_blocks)

    if neighbours == group - 1 and group & (group - 1) == 0:
        half = group // 2

        def place(m):
            return lambda g: ((g ^ m) - g + middle) & (group - 1)

        def entry_of(d, g):
            return ((g + d - middle) & (group - 1)) ^ g

        count = group
        across = move(packed, "grp", lambda g: g ^ half)
        if True:
            across, left = lax.optimization_barrier((across, left))
        pair = jnp.stack([packed, across])
        parts_in = [([packed], [[0]])]
        order = (3, 2, 1)
        for m in order:
            came = move(pair, "grp", lambda g, m=m: g ^ m)
            parts_in.append(([came], [[m, m ^ half]]))
        late = 1
        cut = len(parts_in) - late
        groups = [parts_in[:cut], parts_in[cut:]] if late else [parts_in]
    else:

        def place(d):
            return lambda g: d

        def entry_of(d, g):
            return d

        count = neighbours
        parts_in = [([packed], [[middle]])]
        for k in range(1, middle + 1):
            for s in (k, -k):
                came = move(packed, "grp", lambda g, s=s: (g - s) % group)
                parts_in.append(([came], [[middle + s]]))
        groups = [parts_in]

    owns, priors, counts = [], [], []
    for members in groups:
        arrays = [a for came, _ in members for a in came]
        entries = [es for _, lists in members for es in lists]
        plan = [[place(e) for e in es] for es in entries]
        flat = [e for es in entries for e in es]
        own, onward = pl.pallas_call(
            functools.partial(product_kernel, plan),
            out_shape=[
                pltpu.VMEM((len(flat), size, 2 * size), jnp.float32),
                pltpu.VMEM((len(flat), size, 2 * size), jnp.bfloat16),
            ],
            in_specs=[VMEM] * (len(arrays) + 1),
            out_specs=[VMEM] * 2,
        )(near(left), *[near(a) for a in arrays])
        owns.append(own)
        priors.append(move(onward, "blk", lambda b: (b + 1) % parts))
        counts.append(flat)
    return pl.pallas_call(
        functools.partial(output_kernel, entry_of, neighbours, counts),
        out_shape=jax.ShapeDtypeStruct((size, neighbours * 3 * size), jnp.bfloat16),
        in_specs=[VMEM] * (2 * len(counts)),
        out_specs=VMEM,
        scratch_shapes=[pltpu.VMEM((count, size, 2 * size), jnp.float32)] * 2,
    )(*[near(p) for p in priors], *[near(o) for o in owns])


def solution(mesh):
    in_specs = (
        P(("blk", "grp"), None, None, None),
        P(("blk", "grp"), None),
        P(("blk", "grp"), None, None),
        P(("blk", "grp"), None, None, None),
        P(("blk", "grp")),
    )
    out_specs = P(("blk", "grp"), None)
    return jax.shard_map(shards, mesh=mesh, in_specs=in_specs, out_specs=out_specs, check_vma=False)
```

```python
import functools

import jax
import jax.numpy as jnp
from jax import lax
from jax.experimental import pallas as pl
from jax.experimental.pallas import tpu as pltpu
from jax.sharding import PartitionSpec as P

VMEM = pl.BlockSpec(memory_space=pltpu.VMEM)
SMEM = pl.BlockSpec(memory_space=pltpu.SMEM)


def near(value):
    return pltpu.with_memory_space_constraint(value, pltpu.VMEM)


def pack_kernel(mask_ref, p_ref, out_ref):
    rows, _, size, _ = p_ref.shape
    for r in range(rows):
        second = p_ref[r, 1].astype(jnp.float32) * mask_ref[r].astype(jnp.float32)
        out_ref[r * size : (r + 1) * size, :] = jnp.concatenate(
            [p_ref[r, 0], second.astype(jnp.bfloat16)], axis=1
        )


def left_kernel(slot_ref, wanted_ref, packed_ref, a_ref, out_ref, *sums):
    rows, stencil, size, _ = a_ref.shape
    caps = wanted_ref.shape[0]
    for r in range(rows):
        sums[r][...] = jnp.zeros_like(sums[r])
    for k in range(stencil):
        for r in range(rows):
            slot = slot_ref[r, k]
            place, c = slot // caps, slot % caps
            t = place * rows + wanted_ref[c, place]
            sums[r][t] += a_ref[r, k].astype(jnp.float32)
    turned = packed_ref[...].T
    for d in range(out_ref.shape[0]):
        x = jnp.concatenate(
            [
                jnp.concatenate([sums[r][d * rows + q] for r in range(rows)], axis=0)
                for q in range(rows)
            ],
            axis=1,
        )
        high = x.astype(jnp.bfloat16)
        low = (x - high.astype(jnp.float32)).astype(jnp.bfloat16)
        value = jnp.dot(turned, high, preferred_element_type=jnp.float32)
        value += jnp.dot(turned, low, preferred_element_type=jnp.float32)
        out_ref[d] = value.astype(jnp.bfloat16)


def product_kernel(plan, left_ref, *refs):
    own_ref, next_ref = refs[-2:]
    size = own_ref.shape[1]
    g = lax.axis_index("grp")
    at = 0
    for places, ref in zip(plan, refs[:-2]):
        for i, place in enumerate(places):
            factor = ref[...] if len(ref.shape) == 2 else ref[i]
            value = jnp.dot(left_ref[place(g)], factor, preferred_element_type=jnp.float32)
            own_ref[at] = value[:size]
            next_ref[at] = value[size:].astype(jnp.bfloat16)
            at += 1


def output_kernel(entry_of, neighbours, counts, *refs):
    pieces, owns = refs[: len(counts)], refs[len(counts) : 2 * len(counts)]
    out_ref, prior, own = refs[2 * len(counts) :]
    size, width = own.shape[1:]
    half = width // 2
    lower = lax.broadcasted_iota(jnp.int32, (size, width), 1) < half
    g = lax.axis_index("grp")
    for piece, mine, entries in zip(pieces, owns, counts):
        for i, e in enumerate(entries):
            prior[e] = piece[i].astype(jnp.float32)
            own[e] = mine[i]
    for d in range(0, neighbours, 2):
        at = d * 3 * half
        e = entry_of(d, g)
        x, o = prior[e], own[e]
        turned = pltpu.roll(o, half, 1)
        first = jnp.where(lower, x, x + turned)
        out_ref[:, at : at + width] = first.astype(jnp.bfloat16)
        if d + 1 < neighbours:
            e = entry_of(d + 1, g)
            y, q = prior[e], own[e]
            moved = pltpu.roll(y, half, 1)
            second = jnp.where(lower, turned, moved)
            third = jnp.where(lower, q + moved, q)
            out_ref[:, at + width : at + 2 * width] = second.astype(jnp.bfloat16)
            out_ref[:, at + 2 * width : at + 3 * width] = third.astype(jnp.bfloat16)
        else:
            out_ref[:, at + width : at + 3 * half] = turned[:, :half].astype(jnp.bfloat16)


def shards(a_blocks, a_slot, import_rows, p_blocks, next_mask):
    rows, stencil, size, _ = a_blocks.shape
    neighbours = import_rows.shape[1]
    middle = neighbours // 2
    group, parts = lax.axis_size("grp"), lax.axis_size("blk")

    def move(value, axis, place):
        route = [(i, place(i)) for i in range(lax.axis_size(axis))]
        return lax.ppermute(value, axis, route)

    packed = pl.pallas_call(
        pack_kernel,
        out_shape=pltpu.VMEM((rows * size, 2 * size), jnp.bfloat16),
        in_specs=[SMEM, VMEM],
        out_specs=VMEM,
    )(next_mask, p_blocks)
    left = pl.pallas_call(
        left_kernel,
        out_shape=pltpu.VMEM((neighbours, 2 * size, rows * size), jnp.bfloat16),
        in_specs=[SMEM, SMEM, VMEM, VMEM],
        out_specs=VMEM,
        scratch_shapes=[pltpu.VMEM((neighbours * rows, size, size), jnp.float32)] * rows,
    )(a_slot, import_rows[0].T, near(packed), a_blocks)

    if neighbours == group - 1 and group & (group - 1) == 0:
        half = group // 2

        def place(m):
            return lambda g: ((g ^ m) - g + middle) & (group - 1)

        def entry_of(d, g):
            return ((g + d - middle) & (group - 1)) ^ g

        count = group
        first, single = half + half // 2, half // 2
        across = move(packed, "grp", lambda g: g ^ first)
        across, left = lax.optimization_barrier((across, left))
        pair = jnp.stack([packed, across])
        parts_in = [([packed, across], [[0], [first]])]
        for m in [m for m in range(half - 1, 0, -1) if m != single]:
            came = move(pair, "grp", lambda g, m=m: g ^ m)
            parts_in.append(([came], [[m, m ^ first]]))
        came = move(packed, "grp", lambda g: g ^ single)
        parts_in.append(([came], [[single]]))
        groups = [parts_in[:2], parts_in[2:]]
    else:

        def place(d):
            return lambda g: d

        def entry_of(d, g):
            return d

        count = neighbours
        parts_in = [([packed], [[middle]])]
        for k in range(1, middle + 1):
            for s in (k, -k):
                came = move(packed, "grp", lambda g, s=s: (g - s) % group)
                parts_in.append(([came], [[middle + s]]))
        groups = [parts_in]

    owns, priors, counts = [], [], []
    for members in groups:
        arrays = [a for came, _ in members for a in came]
        entries = [es for _, lists in members for es in lists]
        plan = [[place(e) for e in es] for es in entries]
        flat = [e for es in entries for e in es]
        own, onward = pl.pallas_call(
            functools.partial(product_kernel, plan),
            out_shape=[
                pltpu.VMEM((len(flat), size, 2 * size), jnp.float32),
                pltpu.VMEM((len(flat), size, 2 * size), jnp.bfloat16),
            ],
            in_specs=[VMEM] * (len(arrays) + 1),
            out_specs=[VMEM] * 2,
        )(near(left), *[near(a) for a in arrays])
        owns.append(own)
        priors.append(move(onward, "blk", lambda b: (b + 1) % parts))
        counts.append(flat)
    return pl.pallas_call(
        functools.partial(output_kernel, entry_of, neighbours, counts),
        out_shape=jax.ShapeDtypeStruct((size, neighbours * 3 * size), jnp.bfloat16),
        in_specs=[VMEM] * (2 * len(counts)),
        out_specs=VMEM,
        scratch_shapes=[pltpu.VMEM((count, size, 2 * size), jnp.float32)] * 2,
    )(*[near(p) for p in priors], *[near(o) for o in owns])


def solution(mesh):
    in_specs = (
        P(("blk", "grp"), None, None, None),
        P(("blk", "grp"), None),
        P(("blk", "grp"), None, None),
        P(("blk", "grp"), None, None, None),
        P(("blk", "grp")),
    )
    out_specs = P(("blk", "grp"), None)
    return jax.shard_map(shards, mesh=mesh, in_specs=in_specs, out_specs=out_specs, check_vma=False)
```

```python
import functools

import jax
import jax.numpy as jnp
from jax import lax
from jax.experimental import pallas as pl
from jax.experimental.pallas import tpu as pltpu
from jax.sharding import PartitionSpec as P

VMEM = pl.BlockSpec(memory_space=pltpu.VMEM)
SMEM = pl.BlockSpec(memory_space=pltpu.SMEM)


def near(value):
    return pltpu.with_memory_space_constraint(value, pltpu.VMEM)


def pack_kernel(mask_ref, p_ref, out_ref):
    rows, _, size, _ = p_ref.shape
    for r in range(rows):
        second = p_ref[r, 1].astype(jnp.float32) * mask_ref[r].astype(jnp.float32)
        out_ref[r * size : (r + 1) * size, :] = jnp.concatenate(
            [p_ref[r, 0], second.astype(jnp.bfloat16)], axis=1
        )


def left_kernel(slot_ref, wanted_ref, packed_ref, a_ref, out_ref, *sums):
    rows, stencil, size, _ = a_ref.shape
    caps = wanted_ref.shape[0]
    for r in range(rows):
        sums[r][...] = jnp.zeros_like(sums[r])
    for k in range(stencil):
        for r in range(rows):
            slot = slot_ref[r, k]
            place, c = slot // caps, slot % caps
            t = place * rows + wanted_ref[c, place]
            sums[r][t] += a_ref[r, k].astype(jnp.float32)
    turned = packed_ref[...].T
    for d in range(out_ref.shape[0]):
        x = jnp.concatenate(
            [
                jnp.concatenate([sums[r][d * rows + q] for r in range(rows)], axis=0)
                for q in range(rows)
            ],
            axis=1,
        )
        high = x.astype(jnp.bfloat16)
        low = (x - high.astype(jnp.float32)).astype(jnp.bfloat16)
        value = jnp.dot(turned, high, preferred_element_type=jnp.float32)
        value += jnp.dot(turned, low, preferred_element_type=jnp.float32)
        out_ref[d] = value.astype(jnp.bfloat16)


def product_kernel(plan, left_ref, *refs):
    own_ref, next_ref = refs[-2:]
    size = own_ref.shape[1]
    g = lax.axis_index("grp")
    at = 0
    for places, ref in zip(plan, refs[:-2]):
        for i, place in enumerate(places):
            factor = ref[...] if len(ref.shape) == 2 else ref[i]
            value = jnp.dot(left_ref[place(g)], factor, preferred_element_type=jnp.float32)
            own_ref[at] = value[:size]
            next_ref[at] = value[size:].astype(jnp.bfloat16)
            at += 1


def output_kernel(entry_of, neighbours, counts, *refs):
    pieces, owns = refs[: len(counts)], refs[len(counts) : 2 * len(counts)]
    out_ref, prior, own = refs[2 * len(counts) :]
    size, width = own.shape[1:]
    half = width // 2
    lower = lax.broadcasted_iota(jnp.int32, (size, width), 1) < half
    g = lax.axis_index("grp")
    for piece, mine, entries in zip(pieces, owns, counts):
        for i, e in enumerate(entries):
            prior[e] = piece[i].astype(jnp.float32)
            own[e] = mine[i]
    for d in range(0, neighbours, 2):
        at = d * 3 * half
        e = entry_of(d, g)
        x, o = prior[e], own[e]
        turned = pltpu.roll(o, half, 1)
        first = jnp.where(lower, x, x + turned)
        out_ref[:, at : at + width] = first.astype(jnp.bfloat16)
        if d + 1 < neighbours:
            e = entry_of(d + 1, g)
            y, q = prior[e], own[e]
            moved = pltpu.roll(y, half, 1)
            second = jnp.where(lower, turned, moved)
            third = jnp.where(lower, q + moved, q)
            out_ref[:, at + width : at + 2 * width] = second.astype(jnp.bfloat16)
            out_ref[:, at + 2 * width : at + 3 * width] = third.astype(jnp.bfloat16)
        else:
            out_ref[:, at + width : at + 3 * half] = turned[:, :half].astype(jnp.bfloat16)


def shards(a_blocks, a_slot, import_rows, p_blocks, next_mask):
    rows, stencil, size, _ = a_blocks.shape
    neighbours = import_rows.shape[1]
    middle = neighbours // 2
    group, parts = lax.axis_size("grp"), lax.axis_size("blk")

    def move(value, axis, place):
        route = [(i, place(i)) for i in range(lax.axis_size(axis))]
        return lax.ppermute(value, axis, route)

    packed = pl.pallas_call(
        pack_kernel,
        out_shape=pltpu.VMEM((rows * size, 2 * size), jnp.bfloat16),
        in_specs=[SMEM, VMEM],
        out_specs=VMEM,
    )(next_mask, p_blocks)
    left = pl.pallas_call(
        left_kernel,
        out_shape=pltpu.VMEM((neighbours, 2 * size, rows * size), jnp.bfloat16),
        in_specs=[SMEM, SMEM, VMEM, VMEM],
        out_specs=VMEM,
        scratch_shapes=[pltpu.VMEM((neighbours * rows, size, size), jnp.float32)] * rows,
    )(a_slot, import_rows[0].T, near(packed), a_blocks)

    if neighbours == group - 1 and group & (group - 1) == 0:
        half = group // 2

        def place(m):
            return lambda g: ((g ^ m) - g + middle) & (group - 1)

        def entry_of(d, g):
            return ((g + d - middle) & (group - 1)) ^ g

        count = group
        first = half + half // 2
        across = move(packed, "grp", lambda g: g ^ first)
        parts_in = [([packed, across], [[0], [first]])]
        for m in [m for m in range(group - 2, 1, -1) if m not in (half, first)]:
            came = move(packed, "grp", lambda g, m=m: g ^ m)
            parts_in.append(([came], [[m]]))
        came = move(jnp.stack([packed, across]), "grp", lambda g: g ^ 1)
        parts_in.append(([came], [[1, 1 ^ first]]))
        groups = [parts_in[:-1], parts_in[-1:]]
    else:

        def place(d):
            return lambda g: d

        def entry_of(d, g):
            return d

        count = neighbours
        parts_in = [([packed], [[middle]])]
        for k in range(1, middle + 1):
            for s in (k, -k):
                came = move(packed, "grp", lambda g, s=s: (g - s) % group)
                parts_in.append(([came], [[middle + s]]))
        groups = [parts_in]

    owns, priors, counts = [], [], []
    for members in groups:
        arrays = [a for came, _ in members for a in came]
        entries = [es for _, lists in members for es in lists]
        plan = [[place(e) for e in es] for es in entries]
        flat = [e for es in entries for e in es]
        own, onward = pl.pallas_call(
            functools.partial(product_kernel, plan),
            out_shape=[
                pltpu.VMEM((len(flat), size, 2 * size), jnp.float32),
                pltpu.VMEM((len(flat), size, 2 * size), jnp.bfloat16),
            ],
            in_specs=[VMEM] * (len(arrays) + 1),
            out_specs=[VMEM] * 2,
        )(near(left), *[near(a) for a in arrays])
        owns.append(own)
        priors.append(move(onward, "blk", lambda b: (b + 1) % parts))
        counts.append(flat)
    return pl.pallas_call(
        functools.partial(output_kernel, entry_of, neighbours, counts),
        out_shape=jax.ShapeDtypeStruct((size, neighbours * 3 * size), jnp.bfloat16),
        in_specs=[VMEM] * (2 * len(counts)),
        out_specs=VMEM,
        scratch_shapes=[pltpu.VMEM((count, size, 2 * size), jnp.float32)] * 2,
    )(*[near(p) for p in priors], *[near(o) for o in owns])


def solution(mesh):
    in_specs = (
        P(("blk", "grp"), None, None, None),
        P(("blk", "grp"), None),
        P(("blk", "grp"), None, None),
        P(("blk", "grp"), None, None, None),
        P(("blk", "grp")),
    )
    out_specs = P(("blk", "grp"), None)
    return jax.shard_map(shards, mesh=mesh, in_specs=in_specs, out_specs=out_specs, check_vma=False)
```

```python
import functools

import jax
import jax.numpy as jnp
from jax import lax
from jax.experimental import pallas as pl
from jax.experimental.pallas import tpu as pltpu
from jax.sharding import PartitionSpec as P

VMEM = pl.BlockSpec(memory_space=pltpu.VMEM)
SMEM = pl.BlockSpec(memory_space=pltpu.SMEM)
HBM = pl.BlockSpec(memory_space=pl.ANY)


def near(value):
    return pltpu.with_memory_space_constraint(value, pltpu.VMEM)


def pack_kernel(mask_ref, p_ref, out_ref):
    rows, _, size, _ = p_ref.shape
    for r in range(rows):
        second = p_ref[r, 1].astype(jnp.float32) * mask_ref[r].astype(jnp.float32)
        out_ref[r * size : (r + 1) * size, :] = jnp.concatenate(
            [p_ref[r, 0], second.astype(jnp.bfloat16)], axis=1
        )


def left_kernel(slot_hbm, wanted_hbm, packed_ref, a_hbm, out_ref, slots, wanted, a_ref, sems, *sums):
    rows, stencil, size, _ = a_ref.shape
    caps = wanted.shape[0]
    first = pltpu.make_async_copy(slot_hbm, slots, sems.at[0])
    second = pltpu.make_async_copy(wanted_hbm, wanted, sems.at[1])
    first.start()
    second.start()
    step = pl.cdiv(stencil, sems.shape[0] - 2)
    copies = []
    for i, at in enumerate(range(0, stencil, step)):
        part = pl.ds(at, min(step, stencil - at))
        copies.append(pltpu.make_async_copy(a_hbm.at[:, part], a_ref.at[:, part], sems.at[i + 2]))
        copies[-1].start()
    for r in range(rows):
        sums[r][...] = jnp.zeros_like(sums[r])
    turned = packed_ref[...].T
    first.wait()
    second.wait()
    for k in range(stencil):
        if k % step == 0:
            copies[k // step].wait()
        for r in range(rows):
            slot = slots[r, k]
            place, c = slot // caps, slot % caps
            t = place * rows + wanted[c, place]
            sums[r][t] += a_ref[r, k].astype(jnp.float32)
    for d in range(out_ref.shape[0]):
        x = jnp.concatenate(
            [
                jnp.concatenate([sums[r][d * rows + q] for r in range(rows)], axis=0)
                for q in range(rows)
            ],
            axis=1,
        )
        high = x.astype(jnp.bfloat16)
        low = (x - high.astype(jnp.float32)).astype(jnp.bfloat16)
        value = jnp.dot(turned, high, preferred_element_type=jnp.float32)
        value += jnp.dot(turned, low, preferred_element_type=jnp.float32)
        out_ref[d] = value.astype(jnp.bfloat16)


def product_kernel(plan, late, left_ref, *refs):
    own_ref, next_ref = refs[-2:]
    size = own_ref.shape[1]
    g = lax.axis_index("grp")
    at = 0
    for places, ref in zip(plan, refs[:-2]):
        for i, place in enumerate(places):
            factor = ref[...] if len(ref.shape) == 2 else ref[i]
            value = jnp.dot(left_ref[place(g)], factor, preferred_element_type=jnp.float32)
            own_ref[at] = value[:size]
            next_ref[at] = value[size:].astype(jnp.bfloat16)
            at += 1
    for i, place in enumerate(late):
        next_ref[at + i] = left_ref[place(g), size:]


def late_kernel(late, onward_ref, pair_ref, left_ref, own_ref, kept_ref):
    size = own_ref.shape[1]
    g = lax.axis_index("grp")
    for i, place in enumerate(late):
        own_ref[i] = jnp.dot(
            left_ref[place(g), :size], pair_ref[i], preferred_element_type=jnp.float32
        )
    kept_ref[...] = onward_ref[...]


def output_kernel(entry_of, neighbours, entries, late, came_ref, mine_ref, *refs):
    out_ref, prior, own = refs[-3:]
    size, width = own.shape[1:]
    half = width // 2
    lower = lax.broadcasted_iota(jnp.int32, (size, width), 1) < half
    g = lax.axis_index("grp")
    for i, e in enumerate(entries):
        prior[e] = came_ref[i].astype(jnp.float32)
        own[e] = mine_ref[i]
    for i, e in enumerate(late):
        mine_late, prior_pair = refs[:2]
        prior[e] = jnp.dot(
            came_ref[len(entries) + i], prior_pair[i], preferred_element_type=jnp.float32
        )
        own[e] = mine_late[i]
    for d in range(0, neighbours, 2):
        at = d * 3 * half
        e = entry_of(d, g)
        x, o = prior[e], own[e]
        turned = pltpu.roll(o, half, 1)
        first = jnp.where(lower, x, x + turned)
        out_ref[:, at : at + width] = first.astype(jnp.bfloat16)
        if d + 1 < neighbours:
            e = entry_of(d + 1, g)
            y, q = prior[e], own[e]
            moved = pltpu.roll(y, half, 1)
            second = jnp.where(lower, turned, moved)
            third = jnp.where(lower, q + moved, q)
            out_ref[:, at + width : at + 2 * width] = second.astype(jnp.bfloat16)
            out_ref[:, at + 2 * width : at + 3 * width] = third.astype(jnp.bfloat16)
        else:
            out_ref[:, at + width : at + 3 * half] = turned[:, :half].astype(jnp.bfloat16)


def shards(a_blocks, a_slot, import_rows, p_blocks, next_mask):
    rows, stencil, size, _ = a_blocks.shape
    neighbours = import_rows.shape[1]
    middle = neighbours // 2
    group, parts = lax.axis_size("grp"), lax.axis_size("blk")

    def move(value, axis, place):
        route = [(i, place(i)) for i in range(lax.axis_size(axis))]
        return lax.ppermute(value, axis, route)

    packed = pl.pallas_call(
        pack_kernel,
        out_shape=pltpu.VMEM((rows * size, 2 * size), jnp.bfloat16),
        in_specs=[SMEM, VMEM],
        out_specs=VMEM,
    )(next_mask, p_blocks)
    left = pl.pallas_call(
        left_kernel,
        out_shape=pltpu.VMEM((neighbours, 2 * size, rows * size), jnp.bfloat16),
        in_specs=[HBM, HBM, VMEM, HBM],
        cost_estimate=pl.CostEstimate(flops=2_000_000_000, transcendentals=0, bytes_accessed=0),
        out_specs=VMEM,
        scratch_shapes=[
            pltpu.SMEM(a_slot.shape, a_slot.dtype),
            pltpu.SMEM(import_rows.shape[:0:-1], import_rows.dtype),
            pltpu.VMEM(a_blocks.shape, a_blocks.dtype),
            pltpu.SemaphoreType.DMA((2 + 3,)),
        ]
        + [pltpu.VMEM((neighbours * rows, size, size), jnp.float32)] * rows,
    )(a_slot, import_rows[0].T, near(packed), a_blocks)

    if neighbours == group - 1 and group & (group - 1) == 0:
        half = group // 2

        def place(m):
            return lambda g: ((g ^ m) - g + middle) & (group - 1)

        def entry_of(d, g):
            return ((g + d - middle) & (group - 1)) ^ g

        count = group
        first = half + half // 2
        across = move(packed, "grp", lambda g: g ^ first)
        came, entries = [packed, across], [0, first]
        for m in range(group - 2, 1, -1):
            if m not in (half, first, 1 ^ first):
                came.append(move(packed, "grp", lambda g, m=m: g ^ m))
                entries.append(m)
        pair = jnp.stack([packed, across])
        late = [1, 1 ^ first]
        onward_pair = lax.ppermute(
            pair,
            ("blk", "grp"),
            [
                (b * group + g, (b + 1) % parts * group + (g ^ 1))
                for b in range(parts)
                for g in range(group)
            ],
        )
        near_pair = move(pair, "grp", lambda g: g ^ 1)
        rest = pl.pallas_call(
            functools.partial(late_kernel, [place(e) for e in late]),
            out_shape=[
                pltpu.VMEM((len(late), size, 2 * size), jnp.float32),
                pltpu.VMEM(pair.shape, pair.dtype),
            ],
            in_specs=[VMEM] * 3,
            out_specs=[VMEM] * 2,
            cost_estimate=pl.CostEstimate(flops=2_000_000_000, transcendentals=0, bytes_accessed=0),
        )(near(onward_pair), near(near_pair), near(left))
    else:

        def place(d):
            return lambda g: d

        def entry_of(d, g):
            return d

        count = neighbours
        came, entries, late, rest = [packed], [middle], [], []
        for k in range(1, middle + 1):
            for s in (k, -k):
                came.append(move(packed, "grp", lambda g, s=s: (g - s) % group))
                entries.append(middle + s)

    sent = len(entries) + len(late)
    own, onward = pl.pallas_call(
        functools.partial(
            product_kernel, [[place(e)] for e in entries], [place(e) for e in late]
        ),
        out_shape=[
            pltpu.VMEM((len(entries), size, 2 * size), jnp.float32),
            pltpu.VMEM((sent, size, 2 * size), jnp.bfloat16),
        ],
        in_specs=[VMEM] * (len(came) + 1),
        out_specs=[VMEM] * 2,
    )(near(left), *[near(c) for c in came])
    prior = move(onward, "blk", lambda b: (b + 1) % parts)
    return pl.pallas_call(
        functools.partial(output_kernel, entry_of, neighbours, entries, late),
        out_shape=jax.ShapeDtypeStruct((size, neighbours * 3 * size), jnp.bfloat16),
        in_specs=[VMEM] * (2 + len(rest)),
        out_specs=VMEM,
        scratch_shapes=[pltpu.VMEM((count, size, 2 * size), jnp.float32)] * 2,
    )(*[near(v) for v in [prior, own, *rest]])


def solution(mesh):
    in_specs = (
        P(("blk", "grp"), None, None, None),
        P(("blk", "grp"), None),
        P(("blk", "grp"), None, None),
        P(("blk", "grp"), None, None, None),
        P(("blk", "grp")),
    )
    out_specs = P(("blk", "grp"), None)
    return jax.shard_map(shards, mesh=mesh, in_specs=in_specs, out_specs=out_specs, check_vma=False)
```

```python
import functools

import jax
import jax.numpy as jnp
from jax import lax
from jax.experimental import pallas as pl
from jax.experimental.pallas import tpu as pltpu
from jax.sharding import PartitionSpec as P

VMEM = pl.BlockSpec(memory_space=pltpu.VMEM)
SMEM = pl.BlockSpec(memory_space=pltpu.SMEM)
HBM = pl.BlockSpec(memory_space=pl.ANY)


def near(value):
    return pltpu.with_memory_space_constraint(value, pltpu.VMEM)


def pack_kernel(mask_ref, p_ref, out_ref):
    rows, _, size, _ = p_ref.shape
    for r in range(rows):
        second = p_ref[r, 1].astype(jnp.float32) * mask_ref[r].astype(jnp.float32)
        out_ref[r * size : (r + 1) * size, :] = jnp.concatenate(
            [p_ref[r, 0], second.astype(jnp.bfloat16)], axis=1
        )


def left_kernel(slot_hbm, wanted_hbm, packed_ref, a_hbm, out_ref, slots, wanted, a_ref, sems, *sums):
    rows, stencil, size, _ = a_ref.shape
    caps = wanted.shape[0]
    first = pltpu.make_async_copy(slot_hbm, slots, sems.at[0])
    second = pltpu.make_async_copy(wanted_hbm, wanted, sems.at[1])
    first.start()
    second.start()
    step = pl.cdiv(stencil, sems.shape[0] - 2)
    copies = []
    for i, at in enumerate(range(0, stencil, step)):
        part = pl.ds(at, min(step, stencil - at))
        copies.append(pltpu.make_async_copy(a_hbm.at[:, part], a_ref.at[:, part], sems.at[i + 2]))
        copies[-1].start()
    for r in range(rows):
        sums[r][...] = jnp.zeros_like(sums[r])
    turned = packed_ref[...].T
    first.wait()
    second.wait()
    for k in range(stencil):
        if k % step == 0:
            copies[k // step].wait()
        for r in range(rows):
            slot = slots[r, k]
            place, c = slot // caps, slot % caps
            t = place * rows + wanted[c, place]
            sums[r][t] += a_ref[r, k].astype(jnp.float32)
    for d in range(out_ref.shape[0]):
        x = jnp.concatenate(
            [
                jnp.concatenate([sums[r][d * rows + q] for r in range(rows)], axis=0)
                for q in range(rows)
            ],
            axis=1,
        )
        high = x.astype(jnp.bfloat16)
        low = (x - high.astype(jnp.float32)).astype(jnp.bfloat16)
        value = jnp.dot(turned, high, preferred_element_type=jnp.float32)
        value += jnp.dot(turned, low, preferred_element_type=jnp.float32)
        out_ref[d] = value.astype(jnp.bfloat16)


def product_kernel(places, late, left_ref, *refs):
    next_ref = refs[-1]
    size = next_ref.shape[1]
    g = lax.axis_index("grp")
    for i, place in enumerate(places):
        value = jnp.dot(
            left_ref[place(g), size:], refs[i][...], preferred_element_type=jnp.float32
        )
        next_ref[i] = value.astype(jnp.bfloat16)
    for i, place in enumerate(late):
        next_ref[len(places) + i] = left_ref[place(g), size:]


def base_kernel(entry_of, place, neighbours, entries, late, left_ref, *refs):
    came, refs = refs[: len(entries)], refs[len(entries) :]
    base_ref, own = refs[2 if late else 0], refs[-1]
    size, width = own.shape[1:]
    half = width // 2
    lower = lax.broadcasted_iota(jnp.int32, (size, width), 1) < half
    g = lax.axis_index("grp")
    if late:
        onward_ref, pair_ref, _, kept_ref = refs[:4]
        kept_ref[...] = onward_ref[...]
    for i, e in enumerate(entries):
        own[e] = jnp.dot(
            left_ref[place(e)(g), :size], came[i][...], preferred_element_type=jnp.float32
        )
    for i, e in enumerate(late):
        own[e] = jnp.dot(
            left_ref[place(e)(g), :size], pair_ref[i], preferred_element_type=jnp.float32
        )
    for d in range(0, neighbours, 2):
        at = d * 3 * half
        turned = pltpu.roll(own[entry_of(d, g)], half, 1)
        base_ref[:, at : at + width] = jnp.where(lower, 0.0, turned)
        if d + 1 < neighbours:
            base_ref[:, at + width : at + 2 * width] = jnp.where(lower, turned, 0.0)
            base_ref[:, at + 2 * width : at + 3 * width] = own[entry_of(d + 1, g)]
        else:
            base_ref[:, at + width : at + 3 * half] = turned[:, :half]


def output_kernel(entry_of, neighbours, entries, late, came_ref, base_ref, *refs):
    out_ref, prior = refs[-2:]
    size, width = prior.shape[1:]
    half = width // 2
    lower = lax.broadcasted_iota(jnp.int32, (size, width), 1) < half
    g = lax.axis_index("grp")
    for i, e in enumerate(entries):
        prior[e] = came_ref[i].astype(jnp.float32)
    for i, e in enumerate(late):
        prior[e] = jnp.dot(
            came_ref[len(entries) + i], refs[0][i], preferred_element_type=jnp.float32
        )
    for d in range(0, neighbours, 2):
        at = d * 3 * half
        blocks = [prior[entry_of(d, g)]]
        if d + 1 < neighbours:
            moved = pltpu.roll(prior[entry_of(d + 1, g)], half, 1)
            blocks += [jnp.where(lower, 0.0, moved), jnp.where(lower, moved, 0.0)]
        for block in blocks:
            value = base_ref[:, at : at + width] + block
            out_ref[:, at : at + width] = value.astype(jnp.bfloat16)
            at += width
    out_ref[:, at:] = base_ref[:, at:].astype(jnp.bfloat16)


def shards(a_blocks, a_slot, import_rows, p_blocks, next_mask):
    rows, stencil, size, _ = a_blocks.shape
    neighbours = import_rows.shape[1]
    middle = neighbours // 2
    group, parts = lax.axis_size("grp"), lax.axis_size("blk")

    def move(value, axis, place):
        route = [(i, place(i)) for i in range(lax.axis_size(axis))]
        return lax.ppermute(value, axis, route)

    packed = pl.pallas_call(
        pack_kernel,
        out_shape=pltpu.VMEM((rows * size, 2 * size), jnp.bfloat16),
        in_specs=[SMEM, VMEM],
        out_specs=VMEM,
    )(next_mask, p_blocks)
    left = pl.pallas_call(
        left_kernel,
        out_shape=pltpu.VMEM((neighbours, 2 * size, rows * size), jnp.bfloat16),
        in_specs=[HBM, HBM, VMEM, HBM],
        cost_estimate=pl.CostEstimate(flops=2_000_000_000, transcendentals=0, bytes_accessed=0),
        out_specs=VMEM,
        scratch_shapes=[
            pltpu.SMEM(a_slot.shape, a_slot.dtype),
            pltpu.SMEM(import_rows.shape[:0:-1], import_rows.dtype),
            pltpu.VMEM(a_blocks.shape, a_blocks.dtype),
            pltpu.SemaphoreType.DMA((2 + 3,)),
        ]
        + [pltpu.VMEM((neighbours * rows, size, size), jnp.float32)] * rows,
    )(a_slot, import_rows[0].T, near(packed), a_blocks)

    if neighbours == group - 1 and group & (group - 1) == 0:
        half = group // 2

        def place(m):
            return lambda g: ((g ^ m) - g + middle) & (group - 1)

        def entry_of(d, g):
            return ((g + d - middle) & (group - 1)) ^ g

        count = group
        first = half + half // 2
        across = move(packed, "grp", lambda g: g ^ first)
        came, entries = [packed, across], [0, first]
        for m in range(group - 2, 1, -1):
            if m not in (half, first, 1 ^ first):
                came.append(move(packed, "grp", lambda g, m=m: g ^ m))
                entries.append(m)
        pair = jnp.stack([packed, across])
        late = [1, 1 ^ first]
        onward_pair = lax.ppermute(
            pair,
            ("blk", "grp"),
            [
                (b * group + g, (b + 1) % parts * group + (g ^ 1))
                for b in range(parts)
                for g in range(group)
            ],
        )
        near_pair = move(pair, "grp", lambda g: g ^ 1)
        rest = [onward_pair, near_pair]
    else:

        def place(d):
            return lambda g: d

        def entry_of(d, g):
            return d

        count = neighbours
        came, entries, late, rest = [packed], [middle], [], []
        for k in range(1, middle + 1):
            for s in (k, -k):
                came.append(move(packed, "grp", lambda g, s=s: (g - s) % group))
                entries.append(middle + s)

    sent = len(entries) + len(late)
    onward = pl.pallas_call(
        functools.partial(product_kernel, [place(e) for e in entries], [place(e) for e in late]),
        out_shape=pltpu.VMEM((sent, size, 2 * size), jnp.bfloat16),
        in_specs=[VMEM] * (len(came) + 1),
        out_specs=VMEM,
    )(near(left), *[near(c) for c in came])
    prior = move(onward, "blk", lambda b: (b + 1) % parts)
    wide = neighbours * 3 * size
    kept = [pltpu.VMEM(rest[0].shape, rest[0].dtype)] if late else []
    made = pl.pallas_call(
        functools.partial(base_kernel, entry_of, place, neighbours, entries, late),
        out_shape=[pltpu.VMEM((size, wide), jnp.float32)] + kept,
        in_specs=[VMEM] * (1 + len(came) + len(rest)),
        out_specs=[VMEM] * (1 + len(kept)),
        scratch_shapes=[pltpu.VMEM((count, size, 2 * size), jnp.float32)],
        cost_estimate=pl.CostEstimate(flops=2_000_000_000, transcendentals=0, bytes_accessed=0),
    )(*[near(v) for v in [left, *came, *rest]])
    return pl.pallas_call(
        functools.partial(output_kernel, entry_of, neighbours, entries, late),
        out_shape=jax.ShapeDtypeStruct((size, wide), jnp.bfloat16),
        in_specs=[VMEM] * (1 + len(made)),
        out_specs=VMEM,
        scratch_shapes=[pltpu.VMEM((count, size, 2 * size), jnp.float32)],
    )(*[near(v) for v in [prior, *made]])


def solution(mesh):
    in_specs = (
        P(("blk", "grp"), None, None, None),
        P(("blk", "grp"), None),
        P(("blk", "grp"), None, None),
        P(("blk", "grp"), None, None, None),
        P(("blk", "grp")),
    )
    out_specs = P(("blk", "grp"), None)
    return jax.shard_map(shards, mesh=mesh, in_specs=in_specs, out_specs=out_specs, check_vma=False)
```

```python
import functools

import jax
import jax.numpy as jnp
from jax import lax
from jax.experimental import pallas as pl
from jax.experimental.pallas import tpu as pltpu
from jax.sharding import PartitionSpec as P

VMEM = pl.BlockSpec(memory_space=pltpu.VMEM)
SMEM = pl.BlockSpec(memory_space=pltpu.SMEM)
HBM = pl.BlockSpec(memory_space=pl.ANY)


def near(value):
    return pltpu.with_memory_space_constraint(value, pltpu.VMEM)


def pack_kernel(mask_ref, p_ref, out_ref):
    rows, _, size, _ = p_ref.shape
    for r in range(rows):
        second = p_ref[r, 1].astype(jnp.float32) * mask_ref[r].astype(jnp.float32)
        out_ref[r * size : (r + 1) * size, :] = jnp.concatenate(
            [p_ref[r, 0], second.astype(jnp.bfloat16)], axis=1
        )


def left_kernel(slot_hbm, wanted_hbm, packed_ref, a_hbm, out_ref, slots, wanted, a_ref, sems, *sums):
    rows, stencil, size, _ = a_ref.shape
    caps = wanted.shape[0]
    first = pltpu.make_async_copy(slot_hbm, slots, sems.at[0])
    second = pltpu.make_async_copy(wanted_hbm, wanted, sems.at[1])
    first.start()
    second.start()
    step = pl.cdiv(stencil, sems.shape[0] - 2)
    copies = []
    for i, at in enumerate(range(0, stencil, step)):
        part = pl.ds(at, min(step, stencil - at))
        copies.append(pltpu.make_async_copy(a_hbm.at[:, part], a_ref.at[:, part], sems.at[i + 2]))
        copies[-1].start()
    for r in range(rows):
        sums[r][...] = jnp.zeros_like(sums[r])
    turned = packed_ref[...].T
    twice = jnp.concatenate([turned, turned], axis=1)
    first.wait()
    second.wait()
    for k in range(stencil):
        if k % step == 0:
            copies[k // step].wait()
        for r in range(rows):
            slot = slots[r, k]
            place, c = slot // caps, slot % caps
            t = place * rows + wanted[c, place]
            sums[r][t] += a_ref[r, k].astype(jnp.float32)
    for d in range(out_ref.shape[0]):
        x = jnp.concatenate(
            [
                jnp.concatenate([sums[r][d * rows + q] for r in range(rows)], axis=0)
                for q in range(rows)
            ],
            axis=1,
        )
        high = x.astype(jnp.bfloat16)
        low = (x - high.astype(jnp.float32)).astype(jnp.bfloat16)
        value = jnp.dot(twice, jnp.concatenate([high, low]), preferred_element_type=jnp.float32)
        out_ref[d] = value.astype(jnp.bfloat16)


def product_kernel(places, late, left_ref, *refs):
    next_ref = refs[-1]
    size = next_ref.shape[1]
    g = lax.axis_index("grp")
    for i, place in enumerate(places):
        value = jnp.dot(
            left_ref[place(g), size:], refs[i][...], preferred_element_type=jnp.float32
        )
        next_ref[i] = value.astype(jnp.bfloat16)
    for i, place in enumerate(late):
        next_ref[len(places) + i] = left_ref[place(g), size:]


def base_kernel(entry_of, place, neighbours, entries, late, left_ref, *refs):
    came, refs = refs[: len(entries)], refs[len(entries) :]
    base_ref, own = refs[2 if late else 0], refs[-1]
    size, width = own.shape[1:]
    half = width // 2
    lower = lax.broadcasted_iota(jnp.int32, (size, width), 1) < half
    g = lax.axis_index("grp")
    if late:
        onward_ref, pair_ref, _, kept_ref = refs[:4]
        kept_ref[...] = onward_ref[...]
    for i, e in enumerate(entries):
        own[e] = jnp.dot(
            left_ref[place(e)(g), :size], came[i][...], preferred_element_type=jnp.float32
        )
    for i, e in enumerate(late):
        own[e] = jnp.dot(
            left_ref[place(e)(g), :size], pair_ref[i], preferred_element_type=jnp.float32
        )
    for d in range(0, neighbours, 2):
        at = d * 3 * half
        turned = pltpu.roll(own[entry_of(d, g)], half, 1)
        base_ref[:, at : at + width] = jnp.where(lower, 0.0, turned)
        if d + 1 < neighbours:
            base_ref[:, at + width : at + 2 * width] = jnp.where(lower, turned, 0.0)
            base_ref[:, at + 2 * width : at + 3 * width] = own[entry_of(d + 1, g)]
        else:
            base_ref[:, at + width : at + 3 * half] = turned[:, :half]


def output_kernel(entry_of, neighbours, entries, late, came_ref, base_ref, *refs):
    out_ref, prior = refs[-2:]
    size, width = prior.shape[1:]
    half = width // 2
    lower = lax.broadcasted_iota(jnp.int32, (size, width), 1) < half
    g = lax.axis_index("grp")
    for i, e in enumerate(entries):
        prior[e] = came_ref[i].astype(jnp.float32)
    for i, e in enumerate(late):
        prior[e] = jnp.dot(
            came_ref[len(entries) + i], refs[0][i], preferred_element_type=jnp.float32
        )
    for d in range(0, neighbours, 2):
        at = d * 3 * half
        blocks = [prior[entry_of(d, g)]]
        if d + 1 < neighbours:
            moved = pltpu.roll(prior[entry_of(d + 1, g)], half, 1)
            blocks += [jnp.where(lower, 0.0, moved), jnp.where(lower, moved, 0.0)]
        for block in blocks:
            value = base_ref[:, at : at + width] + block
            out_ref[:, at : at + width] = value.astype(jnp.bfloat16)
            at += width
    out_ref[:, at:] = base_ref[:, at:].astype(jnp.bfloat16)


def shards(a_blocks, a_slot, import_rows, p_blocks, next_mask):
    rows, stencil, size, _ = a_blocks.shape
    neighbours = import_rows.shape[1]
    middle = neighbours // 2
    group, parts = lax.axis_size("grp"), lax.axis_size("blk")

    def move(value, axis, place):
        route = [(i, place(i)) for i in range(lax.axis_size(axis))]
        return lax.ppermute(value, axis, route)

    packed = pl.pallas_call(
        pack_kernel,
        out_shape=pltpu.VMEM((rows * size, 2 * size), jnp.bfloat16),
        in_specs=[SMEM, VMEM],
        out_specs=VMEM,
    )(next_mask, p_blocks)
    left = pl.pallas_call(
        left_kernel,
        out_shape=pltpu.VMEM((neighbours, 2 * size, rows * size), jnp.bfloat16),
        in_specs=[HBM, HBM, VMEM, HBM],
        cost_estimate=pl.CostEstimate(flops=2_000_000_000, transcendentals=0, bytes_accessed=0),
        out_specs=VMEM,
        scratch_shapes=[
            pltpu.SMEM(a_slot.shape, a_slot.dtype),
            pltpu.SMEM(import_rows.shape[:0:-1], import_rows.dtype),
            pltpu.VMEM(a_blocks.shape, a_blocks.dtype),
            pltpu.SemaphoreType.DMA((2 + 3,)),
        ]
        + [pltpu.VMEM((neighbours * rows, size, size), jnp.float32)] * rows,
    )(a_slot, import_rows[0].T, near(packed), a_blocks)

    if neighbours == group - 1 and group & (group - 1) == 0:
        half = group // 2

        def place(m):
            return lambda g: ((g ^ m) - g + middle) & (group - 1)

        def entry_of(d, g):
            return ((g + d - middle) & (group - 1)) ^ g

        count = group
        first = half + half // 2
        across = move(packed, "grp", lambda g: g ^ first)
        came, entries = [packed, across], [0, first]
        for m in range(group - 2, 1, -1):
            if m not in (half, first, 1 ^ first):
                came.append(move(packed, "grp", lambda g, m=m: g ^ m))
                entries.append(m)
        pair = jnp.stack([packed, across])
        late = [1, 1 ^ first]
        onward_pair = lax.ppermute(
            pair,
            ("blk", "grp"),
            [
                (b * group + g, (b + 1) % parts * group + (g ^ 1))
                for b in range(parts)
                for g in range(group)
            ],
        )
        near_pair = move(pair, "grp", lambda g: g ^ 1)
        rest = [onward_pair, near_pair]
    else:

        def place(d):
            return lambda g: d

        def entry_of(d, g):
            return d

        count = neighbours
        came, entries, late, rest = [packed], [middle], [], []
        for k in range(1, middle + 1):
            for s in (k, -k):
                came.append(move(packed, "grp", lambda g, s=s: (g - s) % group))
                entries.append(middle + s)

    sent = len(entries) + len(late)
    onward = pl.pallas_call(
        functools.partial(product_kernel, [place(e) for e in entries], [place(e) for e in late]),
        out_shape=pltpu.VMEM((sent, size, 2 * size), jnp.bfloat16),
        in_specs=[VMEM] * (len(came) + 1),
        out_specs=VMEM,
    )(near(left), *[near(c) for c in came])
    prior = move(onward, "blk", lambda b: (b + 1) % parts)
    wide = neighbours * 3 * size
    kept = [pltpu.VMEM(rest[0].shape, rest[0].dtype)] if late else []
    made = pl.pallas_call(
        functools.partial(base_kernel, entry_of, place, neighbours, entries, late),
        out_shape=[pltpu.VMEM((size, wide), jnp.float32)] + kept,
        in_specs=[VMEM] * (1 + len(came) + len(rest)),
        out_specs=[VMEM] * (1 + len(kept)),
        scratch_shapes=[pltpu.VMEM((count, size, 2 * size), jnp.float32)],
        cost_estimate=pl.CostEstimate(flops=2_000_000_000, transcendentals=0, bytes_accessed=0),
    )(*[near(v) for v in [left, *came, *rest]])
    return pl.pallas_call(
        functools.partial(output_kernel, entry_of, neighbours, entries, late),
        out_shape=jax.ShapeDtypeStruct((size, wide), jnp.bfloat16),
        in_specs=[VMEM] * (1 + len(made)),
        out_specs=VMEM,
        scratch_shapes=[pltpu.VMEM((count, size, 2 * size), jnp.float32)],
    )(*[near(v) for v in [prior, *made]])


def solution(mesh):
    in_specs = (
        P(("blk", "grp"), None, None, None),
        P(("blk", "grp"), None),
        P(("blk", "grp"), None, None),
        P(("blk", "grp"), None, None, None),
        P(("blk", "grp")),
    )
    out_specs = P(("blk", "grp"), None)
    return jax.shard_map(shards, mesh=mesh, in_specs=in_specs, out_specs=out_specs, check_vma=False)
```
